32 devices in a mesh: wide: 16 (over z, y, x), narrow: 2 (over core).
Axes of the slice: x: 2, y: 2, z: 4, core: 2. Of those that a mesh axis runs over, the one named last changes fastest.
Arguments:
- filt_mean: float32 [128, 128], P(('wide', 'narrow')), may hold values from -6 to 6
- filtered_covariance: float32 [128, 128, 128], P(('wide', 'narrow')), may hold values from -9 to 13, as said below
- noise_cov: float32 [128, 128], replicated, may hold values from -1 to 2, as said below
Outputs:
- smooth_mean: float32 [128, 128], P(('wide', 'narrow'))
- smooth_cov: float32 [128, 128, 128], P(('wide', 'narrow'))
- increment_var: float32 [128, 128], P(('wide', 'narrow'))
The draws below stay inside these ranges and needn't reach their ends.
Inputs may be any that keep to these rules, and one draw needn't show every extreme that they name: `filtered_covariance`: each 128 x 128 slice is symmetric positive definite. `noise_cov`: symmetric positive definite.
All inputs are finite; a program needn't handle non-finite values.
Results may differ from the reference program's by a relative error of at most 0.0003.
Values sent between devices are 32-bit elements; how exact they have to be, the bound alone decides.
A program may use at most 64 MiB of HBM per device.

```python
import jax
import jax.numpy as jnp
from jax import lax

M = 128
HOUR_STEPS = 128


def draw_filtered_covariance(key, part):
    key_factor = jax.random.fold_in(key, 11)
    key_level = jax.random.fold_in(key, 12)
    key_outburst = jax.random.fold_in(key, 13)
    factor = jax.random.truncated_normal(key_factor, -3.0, 3.0, (HOUR_STEPS, M, M), jnp.float32)
    diag_level = jnp.exp(jax.random.uniform(key_level, (HOUR_STEPS, M), jnp.float32, jnp.log(0.5), jnp.log(2.0)))
    wishart = jnp.einsum('tij,tkj->tik', factor, factor) / M
    outburst_hours = jax.random.randint(key_outburst, (3,), 0, HOUR_STEPS)
    inside_outburst = jnp.any(jnp.arange(HOUR_STEPS)[:, None] == outburst_hours[None, :], axis=1)
    outburst_scale = jnp.where(inside_outburst, 0.25 / HOUR_STEPS, 1.0)
    identity_mat = jnp.eye(M, dtype=jnp.float32)
    covariance_sum = wishart + diag_level[:, :, None] * identity_mat[None, :, :]
    return (outburst_scale[:, None, None] * covariance_sum).astype(jnp.float32)


def draw_noise_cov(key, part):
    key_fast = jax.random.fold_in(key, 21)
    key_quick = jax.random.fold_in(key, 22)
    key_slow = jax.random.fold_in(key, 23)
    key_mixing = jax.random.fold_in(key, 24)
    fast_share = 0.5
    fast_mask = jax.random.uniform(key_fast, (M,), jnp.float32) < fast_share
    quick_rate = jnp.exp(jax.random.uniform(key_quick, (M,), jnp.float32, jnp.log(0.05), jnp.log(0.2)))
    slow_rate = jnp.exp(jax.random.uniform(key_slow, (M,), jnp.float32, jnp.log(0.05), jnp.log(0.5))) / HOUR_STEPS
    noise_rate = jnp.where(fast_mask, quick_rate, slow_rate)
    mixing = jax.random.truncated_normal(key_mixing, -3.0, 3.0, (M, M), jnp.float32)
    wishart = jnp.dot(mixing, mixing.T) / M
    root_rate = jnp.sqrt(noise_rate)
    inner_mat = jnp.eye(M, dtype=jnp.float32) + 0.5 * wishart
    return (root_rate[:, None] * inner_mat * root_rate[None, :]).astype(jnp.float32)


def shard_levels(stream_key, extent, split, low, high):
    gain, own = 1.0, jax.random.fold_in(stream_key, 6)
    for axis_at, parts in split:
        steps = jnp.exp(jax.random.uniform(jax.random.fold_in(own, axis_at), (parts,), jnp.float32, low / len(split), high / len(split)))
        gain = gain * jnp.repeat(steps, extent[axis_at] // parts).reshape([-1 if axis == axis_at else 1 for axis in range(len(extent))])
    return gain


def centred(key, extent, deviation, limit, shards=(), kind=jnp.bfloat16):
    drawn = deviation * jax.random.normal(key, extent, jnp.float32)
    if shards:
        drawn = drawn * shard_levels(key, extent, shards, -0.22, 0.18)
    return jnp.clip(drawn, -limit, limit).astype(kind)


def setup_inputs(seed: int = 0) -> dict:
    arg_keys = jax.random.split(jax.random.key(seed), 4)
    return {
        "filt_mean": centred(arg_keys[0], (HOUR_STEPS, M), 1.0, 6.0, ((0, 32),), jnp.float32),
        "filtered_covariance": draw_filtered_covariance(jax.random.fold_in(arg_keys[3], 71), 0),
        "noise_cov": draw_noise_cov(jax.random.fold_in(arg_keys[3], 71), 0),
    }


def product(left, right):
    return jnp.matmul(left, right, precision=lax.Precision.HIGHEST)

def apply_vec(matrix, vector):
    return jnp.einsum('...ij,...j->...i', matrix, vector, precision=lax.Precision.HIGHEST)

def reference(filt_mean, filtered_covariance, noise_cov):
    chol_factor = jnp.linalg.cholesky(filtered_covariance + noise_cov)
    gain_matrix = jnp.swapaxes(jax.scipy.linalg.cho_solve((chol_factor, True), filtered_covariance), 1, 2)
    last_step = jnp.arange(HOUR_STEPS) == HOUR_STEPS - 1
    gain_matrix = jnp.where(last_step[:, None, None], 0.0, gain_matrix)
    offset = filt_mean - apply_vec(gain_matrix, filt_mean)
    residual_cov = filtered_covariance - product(gain_matrix, filtered_covariance)

    def backward(state_next, inputs):
        mean_next, cov_next = state_next
        gain_one, offset_one, resid_one = inputs
        mean_now = offset_one + apply_vec(gain_one, mean_next)
        cov_now = resid_one + product(product(gain_one, cov_next), gain_one.T)
        return ((mean_now, cov_now), (mean_now, cov_now))
    start = (jnp.zeros((M,), jnp.float32), jnp.zeros((M, M), jnp.float32))
    _, (smooth_mean, smooth_cov) = lax.scan(backward, start, (gain_matrix, offset, residual_cov), reverse=True)
    next_mean = jnp.concatenate([smooth_mean[1:], jnp.zeros((1, M), jnp.float32)], axis=0)
    next_cov = jnp.concatenate([smooth_cov[1:], jnp.zeros((1, M, M), jnp.float32)], axis=0)
    change = next_mean - smooth_mean
    cross_term = jnp.sum(next_cov * gain_matrix, axis=2)
    increments = change * change + jnp.diagonal(next_cov, axis1=1, axis2=2) + jnp.diagonal(smooth_cov, axis1=1, axis2=2) - 2.0 * cross_term
    increments = jnp.where(last_step[:, None], 0.0, increments)
    return (smooth_mean, smooth_cov, increments)
```

```python
import functools

import jax
import jax.numpy as jnp
from jax import lax
from jax.experimental import pallas as pl
from jax.experimental.pallas import tpu as pltpu
from jax.sharding import PartitionSpec as P

PANEL = 16
SUB = 8
SCALE = 0.0625


def split(value, parts):
    pieces = []
    for at in range(parts):
        pieces.append(value.astype(jnp.bfloat16))
        if at < parts - 1:
            value = value - pieces[-1].astype(jnp.float32)
    return pieces


PAIRS = {2: ((0, 0), (0, 1), (1, 0)), 3: ((0, 0), (0, 1), (1, 0), (1, 1), (0, 2), (2, 0))}


def dot(left, right, dims, parts):
    lefts, rights = split(left, parts), split(right, parts)
    return lax.dot_general(
        jnp.concatenate([lefts[i] for i, _ in PAIRS[parts]], axis=dims[0]),
        jnp.concatenate([rights[j] for _, j in PAIRS[parts]], axis=dims[1]),
        ((dims[:1], dims[1:]), ((), ())),
        preferred_element_type=jnp.float32,
    )


def product(left, right, parts=2):
    return dot(left, right, (1, 0), parts)


def product_t(left, right, parts=2):
    return dot(left, right, (1, 1), parts)


def gram(left, right):
    return dot(left, right, (0, 0), 3)


def invert_all(mats):
    mats=list(mats)
    width = mats[0].shape[0]
    panel, sub = min(PANEL, width), min(SUB, width)
    lane = lax.broadcasted_iota(jnp.int32, (sub, width), 1)
    row = lax.broadcasted_iota(jnp.int32, (sub, width), 0)
    wide_lane = lax.broadcasted_iota(jnp.int32, (panel, width), 1)
    wide_row = lax.broadcasted_iota(jnp.int32, (panel, width), 0)
    count = len(mats)
    span = lambda v, k: jnp.broadcast_to(v[k : k + 1], v.shape)
    ones_row = [(row == k).astype(jnp.float32) for k in range(sub)]
    for base in range(0, width, panel):
        olds = [mat[base : base + panel] for mat in mats]
        news = [[old[at : at + sub] for at in range(0, panel, sub)] for old in olds]
        for s in range(panel // sub):
            off = base + s * sub
            spread = lambda v: [jnp.broadcast_to(v[:, off + j : off + j + 1], v.shape) for j in range(sub)]
            cols = [spread(new[s]) for new in news]
            others = [[spread(new[r]) if r != s else None for r in range(panel // sub)] for new in news]
            for k in range(sub):
                unit = (lane == off + k).astype(jnp.float32)
                for at in range(count):
                    col = cols[at]
                    inverse = 1.0 / span(col[k], k)
                    factors = (col[k] - ones_row[k]) * inverse
                    new = news[at][s]
                    news[at][s] = new - factors * (span(new, k) + unit)
                    for j in range(k + 1, sub):
                        col[j] = col[j] - factors * span(col[j], k)
            units = (lane == off + row).astype(jnp.float32)
            for at in range(count):
                filled = news[at][s] + units
                rows = [span(filled, j) for j in range(sub)]
                for r in range(panel // sub):
                    if r != s:
                        terms = [others[at][r][j] * rows[j] for j in range(sub)]
                        while len(terms) > 1:
                            terms = [a + b for a, b in zip(terms[::2], terms[1::2])]
                        news[at][r] = news[at][r] - terms[0]
        inside = (wide_lane >= base) & (wide_lane < base + panel)
        eye = (wide_lane == base + wide_row).astype(jnp.float32)
        for at, mat in enumerate(mats):
            signed = jnp.where(wide_lane < base, -olds[at], olds[at])
            signed = jnp.where(inside, 0.0, signed)
            new = jnp.concatenate(news[at], axis=0)
            pieces = [new]
            if base:
                pieces.insert(0, mat[:base])
            if base + panel < width:
                pieces.append(mat[base + panel :])
            mats[at] = jnp.concatenate(pieces, axis=0) - gram(signed, new + eye)
    return mats


def combine(later, earlier):
    late_gain, late_mean, late_cov = later
    early_gain, early_mean, early_cov = earlier
    width = late_gain.shape[0]
    half = product(early_gain, late_cov)
    down = product_t(jnp.concatenate([half, late_mean], axis=0), early_gain)
    return product(early_gain, late_gain), down[width:] + early_mean, down[:width] + early_cov


def apply(state, elem):
    mean, cov = state
    gain, offset, resid = elem
    width = gain.shape[0]
    half = product(gain, cov)
    down = product_t(jnp.concatenate([half, mean], axis=0), gain)
    return down[width:] + offset, down[:width] + resid


def choose(flag, first, second):
    return tuple(jnp.where(flag, a, b) for a, b in zip(first, second))


def keep(ref, elem):
    width = ref.shape[1]
    ref[:width], ref[2 * width :], ref[width : 2 * width] = elem


def take(ref):
    width = ref.shape[1]
    return ref[:width], ref[2 * width :], ref[width : 2 * width]


def kernel(
    sizes, mean_hbm, cov_hbm, noise_hbm, reached, held, gains,
    mean_ref, cov_ref, noise_ref, load_sem, send, recv, send_sem, recv_sem
):
    loads = [
        pltpu.make_async_copy(source, target, load_sem.at[at])
        for at, (source, target) in enumerate(
            ((noise_hbm, noise_ref), (cov_hbm, cov_ref), (mean_hbm, mean_ref))
        )
    ]
    for load in loads:
        load.start()
    steps, width = mean_ref.shape
    levels = []
    for axis in ("narrow", "wide"):
        place = lax.axis_index(axis)
        bit = 1
        while bit < sizes[axis]:
            later = (place // bit) % 2
            levels.append((axis, place + bit - 2 * bit * later, later == 1))
            bit *= 2
        assert bit == sizes[axis]
    if levels:
        barrier = pltpu.get_barrier_semaphore()
        for axis, partner, _ in levels:
            pl.semaphore_signal(
                barrier, inc=1, device_id={axis: partner}, device_id_type=pl.DeviceIdType.MESH
            )

    for load in loads:
        load.wait()
    noise = noise_ref[...]
    inverses = [
        mat * SCALE for mat in invert_all([(cov_ref[t] + noise) * SCALE for t in range(steps)])
    ]
    final = (lax.axis_index("wide") == sizes["wide"] - 1) & (
        lax.axis_index("narrow") == sizes["narrow"] - 1
    )
    for t in range(steps):
        gain = product(cov_ref[t], inverses[t], 3)
        if t == steps - 1:
            gain = jnp.where(final, 0.0, gain)
        resid = product(gain, noise)
        if t == steps - 1:
            resid = jnp.where(final, cov_ref[t], resid)
        mean = jnp.broadcast_to(mean_ref[t : t + 1, :], (8, width))
        gains[t] = gain
        keep(held.at[t], (gain, mean - product_t(mean, gain, 3), resid))

    def scan(first, last):
        if last - first == 1:
            return take(held.at[first]), lambda: None
        middle = (first + last) // 2
        late, late_rest = scan(middle, last)
        early, early_rest = scan(first, middle)
        whole = combine(late, early)

        def rest():
            late_rest()
            early_rest()
            keep(held.at[middle], late)
            for t in range(first + 1, middle):
                keep(held.at[t], combine(take(held.at[middle]), take(held.at[t])))
            keep(held.at[first], whole)

        return whole, rest

    total, rest = scan(0, steps)

    eye = (
        lax.broadcasted_iota(jnp.int32, (width, width), 0)
        == lax.broadcasted_iota(jnp.int32, (width, width), 1)
    ).astype(jnp.float32)
    incoming = None
    copies = []

    def post(at, part, rows):
        axis, partner, _ = levels[at]
        copy = pltpu.make_async_remote_copy(
            src_ref=send.at[at, rows],
            dst_ref=recv.at[at, rows],
            send_sem=send_sem.at[at, part],
            recv_sem=recv_sem.at[at, part],
            device_id={axis: partner},
            device_id_type=pl.DeviceIdType.MESH,
        )
        copy.start()
        copies.append(copy)
        return copy

    def post_gain(at, gain):
        send[at, :width] = gain
        return post(at, 0, pl.ds(0, width))

    def post_state(at, state):
        send[at, 2 * width :], send[at, width : 2 * width] = state
        return post(at, 1, pl.ds(width, width + 8))

    last = len(levels) - 1
    gain_copy = state_copy = other = None
    if levels:
        pl.semaphore_wait(barrier, len(levels))
        if last > 0:
            gain_copy = post_gain(0, total[0])
        state_copy = post_state(0, total[1:])
    rest()
    for at, (_, _, later) in enumerate(levels):
        if at < last:
            gain_copy.wait_recv()
            other_gain = recv[at, :width]
            late_gain = jnp.where(later, total[0], other_gain)
            early_gain = jnp.where(later, other_gain, total[0])
            if at < last - 1:
                joined_gain = product(early_gain, late_gain)
                gain_copy = post_gain(at + 1, joined_gain)
        state_copy.wait_recv()
        other_state = (recv[at, 2 * width :], recv[at, width : 2 * width])
        if at < last:
            late_state = choose(later, total[1:], other_state)
            early_state = choose(later, other_state, total[1:])
            joined = apply(late_state, (early_gain,) + early_state)
            state_copy = post_state(at + 1, joined)
            total = (joined_gain if at < last - 1 else None,) + joined
            other = (other_gain,) + other_state
            if incoming is None:
                blank = (eye, jnp.zeros((8, width), jnp.float32), jnp.zeros_like(eye))
                incoming = choose(later, blank, other)
            else:
                incoming = choose(later, incoming, combine(other, incoming))
    zero_state = (jnp.zeros((8, width), jnp.float32), jnp.zeros((width, width), jnp.float32))
    if not levels:
        state = zero_state
    elif incoming is None:
        state = choose(later, zero_state, other_state)
    else:
        state = choose(later, incoming[1:], apply(other_state, incoming))
    reached[width:], reached[:width] = state
    for copy in copies:
        copy.wait_send()


def finish(sizes, reached, held, gains, out_mean, out_cov, out_inc):
    steps, width = out_mean.shape
    final = (lax.axis_index("wide") == sizes["wide"] - 1) & (
        lax.axis_index("narrow") == sizes["narrow"] - 1
    )
    eye = (
        lax.broadcasted_iota(jnp.int32, (width, width), 0)
        == lax.broadcasted_iota(jnp.int32, (width, width), 1)
    ).astype(jnp.float32)
    state = reached[width:], reached[:width]
    results = [apply(state, take(held.at[t])) for t in range(steps)]
    ones = jnp.ones((8, width), jnp.float32)
    for t in range(steps):
        mean, cov = results[t]
        next_mean, next_cov = results[t + 1] if t < steps - 1 else state
        out_mean[t : t + 1, :] = mean[:1]
        out_cov[t] = cov
        change = next_mean - mean
        spread = product_t(ones, eye * (next_cov + cov) - 2.0 * (next_cov * gains[t]))
        increment = change * change + spread
        if t == steps - 1:
            increment = jnp.where(final, 0.0, increment)
        out_inc[t : t + 1, :] = increment[:1]


def per_device(sizes, filt_mean, filtered_covariance, noise_cov):
    steps, width = filt_mean.shape
    count = sum(size.bit_length() - 1 for size in sizes.values())
    slots = max(count, 1)
    block = (slots, 2 * width + 8, width)
    params = dict(collective_id=0, has_side_effects=True) if count else {}
    vmem = pl.BlockSpec(memory_space=pltpu.VMEM)
    parts = pl.pallas_call(
        functools.partial(kernel, sizes),
        out_shape=(
            jax.ShapeDtypeStruct((width + 8, width), jnp.float32),
            jax.ShapeDtypeStruct((steps,) + block[1:], jnp.float32),
            jax.ShapeDtypeStruct((steps, width, width), jnp.float32),
        ),
        in_specs=[pl.BlockSpec(memory_space=pltpu.HBM)] * 3,
        out_specs=(vmem,) * 3,
        scratch_shapes=[
            pltpu.VMEM((steps, width), jnp.float32),
            pltpu.VMEM((steps, width, width), jnp.float32),
            pltpu.VMEM((width, width), jnp.float32),
            pltpu.SemaphoreType.DMA((3,)),
            pltpu.VMEM(block, jnp.float32),
            pltpu.VMEM(block, jnp.float32),
            pltpu.SemaphoreType.DMA((slots, 2)),
            pltpu.SemaphoreType.DMA((slots, 2)),
        ],
        compiler_params=pltpu.CompilerParams(vmem_limit_bytes=24 << 20, **params),
    )(filt_mean, filtered_covariance, noise_cov)
    return pl.pallas_call(
        functools.partial(finish, sizes),
        out_shape=(
            jax.ShapeDtypeStruct((steps, width), jnp.float32),
            jax.ShapeDtypeStruct((steps, width, width), jnp.float32),
            jax.ShapeDtypeStruct((steps, width), jnp.float32),
        ),
        in_specs=[vmem] * 3,
        out_specs=(vmem,) * 3,
        compiler_params=pltpu.CompilerParams(vmem_limit_bytes=24 << 20),
    )(*parts)


def solution(mesh):
    sizes = {axis: mesh.shape[axis] for axis in ("wide", "narrow")}
    return jax.shard_map(
        functools.partial(per_device, sizes),
        mesh=mesh,
        in_specs=(P(("wide", "narrow"), None), P(("wide", "narrow"), None, None), P()),
        out_specs=(
            P(("wide", "narrow"), None),
            P(("wide", "narrow"), None, None),
            P(("wide", "narrow"), None),
        ),
        check_vma=False,
    )
```

```python
import functools

import jax
import jax.numpy as jnp
from jax import lax
from jax.experimental import pallas as pl
from jax.experimental.pallas import tpu as pltpu
from jax.sharding import PartitionSpec as P

PANEL = 16
SUB = 8
SCALE = 0.0625


def split(value, parts):
    pieces = []
    for at in range(parts):
        pieces.append(value.astype(jnp.bfloat16))
        if at < parts - 1:
            value = value - pieces[-1].astype(jnp.float32)
    return pieces


PAIRS = {2: ((0, 0), (0, 1), (1, 0)), 3: ((0, 0), (0, 1), (1, 0), (1, 1), (0, 2), (2, 0))}


def dot(left, right, dims, parts):
    lefts, rights = split(left, parts), split(right, parts)
    return lax.dot_general(
        jnp.concatenate([lefts[i] for i, _ in PAIRS[parts]], axis=dims[0]),
        jnp.concatenate([rights[j] for _, j in PAIRS[parts]], axis=dims[1]),
        ((dims[:1], dims[1:]), ((), ())),
        preferred_element_type=jnp.float32,
    )


def product(left, right, parts=2):
    return dot(left, right, (1, 0), parts)


def product_t(left, right, parts=2):
    return dot(left, right, (1, 1), parts)


def gram(left, right):
    return dot(left, right, (0, 0), 3)


def invert_all(mats):
    mats=list(mats)
    width = mats[0].shape[0]
    panel, sub = min(PANEL, width), min(SUB, width)
    lane = lax.broadcasted_iota(jnp.int32, (sub, width), 1)
    row = lax.broadcasted_iota(jnp.int32, (sub, width), 0)
    wide_lane = lax.broadcasted_iota(jnp.int32, (panel, width), 1)
    wide_row = lax.broadcasted_iota(jnp.int32, (panel, width), 0)
    count = len(mats)
    span = lambda v, k: jnp.broadcast_to(v[k : k + 1], v.shape)
    ones_row = [(row == k).astype(jnp.float32) for k in range(sub)]
    for base in range(0, width, panel):
        olds = [mat[base : base + panel] for mat in mats]
        news = [[old[at : at + sub] for at in range(0, panel, sub)] for old in olds]
        for s in range(panel // sub):
            off = base + s * sub
            spread = lambda v: [jnp.broadcast_to(v[:, off + j : off + j + 1], v.shape) for j in range(sub)]
            cols = [spread(new[s]) for new in news]
            others = [[spread(new[r]) if r != s else None for r in range(panel // sub)] for new in news]
            for k in range(sub):
                unit = (lane == off + k).astype(jnp.float32)
                for at in range(count):
                    col = cols[at]
                    inverse = 1.0 / span(col[k], k)
                    factors = (col[k] - ones_row[k]) * inverse
                    new = news[at][s]
                    news[at][s] = new - factors * (span(new, k) + unit)
                    for j in range(k + 1, sub):
                        col[j] = col[j] - factors * span(col[j], k)
            units = (lane == off + row).astype(jnp.float32)
            for at in range(count):
                filled = news[at][s] + units
                rows = [span(filled, j) for j in range(sub)]
                for r in range(panel // sub):
                    if r != s:
                        terms = [others[at][r][j] * rows[j] for j in range(sub)]
                        while len(terms) > 1:
                            terms = [a + b for a, b in zip(terms[::2], terms[1::2])]
                        news[at][r] = news[at][r] - terms[0]
        inside = (wide_lane >= base) & (wide_lane < base + panel)
        eye = (wide_lane == base + wide_row).astype(jnp.float32)
        for at, mat in enumerate(mats):
            signed = jnp.where(wide_lane < base, -olds[at], olds[at])
            signed = jnp.where(inside, 0.0, signed)
            new = jnp.concatenate(news[at], axis=0)
            pieces = [new]
            if base:
                pieces.insert(0, mat[:base])
            if base + panel < width:
                pieces.append(mat[base + panel :])
            mats[at] = jnp.concatenate(pieces, axis=0) - gram(signed, new + eye)
    return mats


def combine(later, earlier):
    late_gain, late_mean, late_cov = later
    early_gain, early_mean, early_cov = earlier
    width = late_gain.shape[0]
    half = product(early_gain, late_cov)
    down = product_t(jnp.concatenate([half, late_mean], axis=0), early_gain)
    return product(early_gain, late_gain), down[width:] + early_mean, down[:width] + early_cov


def apply(state, elem):
    mean, cov = state
    gain, offset, resid = elem
    width = gain.shape[0]
    half = product(gain, cov)
    down = product_t(jnp.concatenate([half, mean], axis=0), gain)
    return down[width:] + offset, down[:width] + resid


def choose(flag, first, second):
    return tuple(jnp.where(flag, a, b) for a, b in zip(first, second))


def keep(ref, elem):
    width = ref.shape[1]
    ref[:width], ref[2 * width :], ref[width : 2 * width] = elem


def take(ref):
    width = ref.shape[1]
    return ref[:width], ref[2 * width :], ref[width : 2 * width]


def kernel(
    sizes, mean_hbm, cov_hbm, noise_hbm, reached, held, gains,
    mean_ref, cov_ref, noise_ref, load_sem, send, recv, send_sem, recv_sem
):
    loads = [
        pltpu.make_async_copy(source, target, load_sem.at[at])
        for at, (source, target) in enumerate(
            ((noise_hbm, noise_ref), (cov_hbm, cov_ref), (mean_hbm, mean_ref))
        )
    ]
    for load in loads:
        load.start()
    steps, width = mean_ref.shape
    levels = []
    for axis in ("narrow", "wide"):
        place = lax.axis_index(axis)
        bit = 1
        while bit < sizes[axis]:
            later = (place // bit) % 2
            levels.append((axis, place + bit - 2 * bit * later, later == 1))
            bit *= 2
        assert bit == sizes[axis]
    if levels:
        barrier = pltpu.get_barrier_semaphore()
        for axis, partner, _ in levels:
            pl.semaphore_signal(
                barrier, inc=1, device_id={axis: partner}, device_id_type=pl.DeviceIdType.MESH
            )

    for load in loads:
        load.wait()
    noise = noise_ref[...]
    inverses = [
        mat * SCALE for mat in invert_all([(cov_ref[t] + noise) * SCALE for t in range(steps)])
    ]
    final = (lax.axis_index("wide") == sizes["wide"] - 1) & (
        lax.axis_index("narrow") == sizes["narrow"] - 1
    )
    for t in range(steps):
        gain = product(cov_ref[t], inverses[t], 3)
        if t == steps - 1:
            gain = jnp.where(final, 0.0, gain)
        resid = product(gain, noise)
        if t == steps - 1:
            resid = jnp.where(final, cov_ref[t], resid)
        mean = jnp.broadcast_to(mean_ref[t : t + 1, :], (8, width))
        gains[t] = gain
        keep(held.at[t], (gain, mean - product_t(mean, gain, 3), resid))

    def scan(first, last):
        if last - first == 1:
            return take(held.at[first]), lambda: None
        middle = (first + last) // 2
        late, late_rest = scan(middle, last)
        early, early_rest = scan(first, middle)
        whole = combine(late, early)

        def rest():
            late_rest()
            early_rest()
            keep(held.at[middle], late)
            for t in range(first + 1, middle):
                keep(held.at[t], combine(take(held.at[middle]), take(held.at[t])))
            keep(held.at[first], whole)

        return whole, rest

    total, rest = scan(0, steps)

    eye = (
        lax.broadcasted_iota(jnp.int32, (width, width), 0)
        == lax.broadcasted_iota(jnp.int32, (width, width), 1)
    ).astype(jnp.float32)
    incoming = None
    copies = []

    def post(at, part, rows):
        axis, partner, _ = levels[at]
        copy = pltpu.make_async_remote_copy(
            src_ref=send.at[at, rows],
            dst_ref=recv.at[at, rows],
            send_sem=send_sem.at[at, part],
            recv_sem=recv_sem.at[at, part],
            device_id={axis: partner},
            device_id_type=pl.DeviceIdType.MESH,
        )
        copy.start()
        copies.append(copy)
        return copy

    def post_gain(at, gain):
        send[at, :width] = gain
        return post(at, 0, pl.ds(0, width))

    def post_state(at, state):
        send[at, 2 * width :], send[at, width : 2 * width] = state
        return post(at, 1, pl.ds(width, width + 8))

    last = len(levels) - 1
    gain_copy = state_copy = other = None
    if levels:
        pl.semaphore_wait(barrier, len(levels))
        if last > 0:
            gain_copy = post_gain(0, total[0])
        state_copy = post_state(0, total[1:])
    rest()
    for at, (_, _, later) in enumerate(levels):
        if at < last:
            gain_copy.wait_recv()
            other_gain = recv[at, :width]
            late_gain = jnp.where(later, total[0], other_gain)
            early_gain = jnp.where(later, other_gain, total[0])
            if at < last - 1:
                joined_gain = product(early_gain, late_gain)
                gain_copy = post_gain(at + 1, joined_gain)
        state_copy.wait_recv()
        other_state = (recv[at, 2 * width :], recv[at, width : 2 * width])
        if at < last:
            late_state = choose(later, total[1:], other_state)
            early_state = choose(later, other_state, total[1:])
            joined = apply(late_state, (early_gain,) + early_state)
            state_copy = post_state(at + 1, joined)
            total = (joined_gain if at < last - 1 else None,) + joined
            other = (other_gain,) + other_state
            if incoming is None:
                blank = (eye, jnp.zeros((8, width), jnp.float32), jnp.zeros_like(eye))
                incoming = choose(later, blank, other)
            else:
                incoming = choose(later, incoming, combine(other, incoming))
    zero_state = (jnp.zeros((8, width), jnp.float32), jnp.zeros((width, width), jnp.float32))
    if not levels:
        state = zero_state
    elif incoming is None:
        state = choose(later, zero_state, other_state)
    else:
        state = choose(later, incoming[1:], apply(other_state, incoming))
    reached[width:], reached[:width] = state
    for copy in copies:
        copy.wait_send()


def finish(sizes, reached, held, gains, out_mean, out_cov, out_inc):
    steps, width = out_mean.shape
    final = (lax.axis_index("wide") == sizes["wide"] - 1) & (
        lax.axis_index("narrow") == sizes["narrow"] - 1
    )
    eye = (
        lax.broadcasted_iota(jnp.int32, (width, width), 0)
        == lax.broadcasted_iota(jnp.int32, (width, width), 1)
    ).astype(jnp.float32)
    state = reached[width:], reached[:width]
    results = [apply(state, take(held.at[t])) for t in range(steps)]
    ones = jnp.ones((8, width), jnp.float32)
    for t in range(steps):
        mean, cov = results[t]
        next_mean, next_cov = results[t + 1] if t < steps - 1 else state
        out_mean[t : t + 1, :] = mean[:1]
        out_cov[t] = cov
        change = next_mean - mean
        spread = product_t(ones, eye * (next_cov + cov) - 2.0 * (next_cov * gains[t]))
        increment = change * change + spread
        if t == steps - 1:
            increment = jnp.where(final, 0.0, increment)
        out_inc[t : t + 1, :] = increment[:1]


def per_device(sizes, filt_mean, filtered_covariance, noise_cov):
    steps, width = filt_mean.shape
    count = sum(size.bit_length() - 1 for size in sizes.values())
    slots = max(count, 1)
    block = (slots, 2 * width + 8, width)
    params = dict(collective_id=0, has_side_effects=True) if count else {}
    vmem = pl.BlockSpec(memory_space=pltpu.VMEM)
    parts = pl.pallas_call(
        functools.partial(kernel, sizes),
        out_shape=(
            jax.ShapeDtypeStruct((width + 8, width), jnp.float32),
            jax.ShapeDtypeStruct((steps,) + block[1:], jnp.float32),
            jax.ShapeDtypeStruct((steps, width, width), jnp.float32),
        ),
        in_specs=[pl.BlockSpec(memory_space=pltpu.HBM)] * 3,
        out_specs=(vmem,) * 3,
        scratch_shapes=[
            pltpu.VMEM((steps, width), jnp.float32),
            pltpu.VMEM((steps, width, width), jnp.float32),
            pltpu.VMEM((width, width), jnp.float32),
            pltpu.SemaphoreType.DMA((3,)),
            pltpu.VMEM(block, jnp.float32),
            pltpu.VMEM(block, jnp.float32),
            pltpu.SemaphoreType.DMA((slots, 2)),
            pltpu.SemaphoreType.DMA((slots, 2)),
        ],
        compiler_params=pltpu.CompilerParams(vmem_limit_bytes=24 << 20, **params),
    )(
        *(
            pltpu.with_memory_space_constraint(value, pltpu.HBM)
            for value in (filt_mean, filtered_covariance, noise_cov)
        )
    )
    return pl.pallas_call(
        functools.partial(finish, sizes),
        out_shape=(
            jax.ShapeDtypeStruct((steps, width), jnp.float32),
            jax.ShapeDtypeStruct((steps, width, width), jnp.float32),
            jax.ShapeDtypeStruct((steps, width), jnp.float32),
        ),
        in_specs=[vmem] * 3,
        out_specs=(vmem,) * 3,
        compiler_params=pltpu.CompilerParams(vmem_limit_bytes=24 << 20),
    )(*parts)


def solution(mesh):
    sizes = {axis: mesh.shape[axis] for axis in ("wide", "narrow")}
    return jax.shard_map(
        functools.partial(per_device, sizes),
        mesh=mesh,
        in_specs=(P(("wide", "narrow"), None), P(("wide", "narrow"), None, None), P()),
        out_specs=(
            P(("wide", "narrow"), None),
            P(("wide", "narrow"), None, None),
            P(("wide", "narrow"), None),
        ),
        check_vma=False,
    )
```
